256 devices in a mesh: mode: 8 (over z_lo, x), space: 32 (over z_hi, y, core).
Axes of the slice: x: 4, y: 4, z: 8 (z_hi: 4, z_lo: 2; z = z_hi * 2 + z_lo), core: 2. Of those that a mesh axis runs over, the one named last changes fastest.
Arguments:
- field: bfloat16 [256, 512, 1024], P('mode', 'space'), may hold values from -6 to 6
- kappa_x: float32 [8, 512, 1024], P(None, 'space'), may hold values from -4 to 4
- kappa_y: float32 [8, 512, 1024], P(None, 'space'), may hold values from -4 to 4
- coupling: bfloat16 [16, 8, 32, 32], P('mode'), may hold values from -0.625 to 0.625
- pattern: int32 [16, 8, 32, 32], P('mode'), may hold values 0 or 1
Outputs:
- image: float32 [256, 512, 1024], P('mode', 'space')
The draws below stay inside these ranges and needn't reach their ends.
All inputs are finite; a program needn't handle non-finite values. No bound on the sum of `pattern` on one device may be relied on, other than what follows from the above.
Results may differ from the reference program's by a relative error of at most 0.0003.
Values may be sent and summed in bfloat16 or wider, within the bound.
No kernel may reach another device: no remote copies, remote signals or barrier semaphores. Data moves between devices by JAX's collectives and lax.ppermute only.
A program may use at most 64 MiB of HBM per device.

```python
import jax
import jax.numpy as jnp
from jax import lax

MB = 32
K = 8
ROUNDS = 1
NY = 1024
MODES = 256
NX = 512
N_MODE = 8


def place_ends(values, rng, least, high):
    place = [jax.random.randint(jax.random.fold_in(rng, axis), (), 0, length) for axis, length in enumerate(values.shape)]
    main_axis = values.shape.index(max(values.shape))
    beside = place[:main_axis] + [(place[main_axis] + 1) % values.shape[main_axis]] + place[main_axis + 1:]
    return values.at[tuple(place)].set(least).at[tuple(beside)].set(high)


def shard_levels(stream_key, dims, pieces, low, high):
    gain = 1.0
    for axis_at, shards_of in pieces:
        steps = jax.random.uniform(jax.random.fold_in(jax.random.fold_in(stream_key, 6), axis_at), (shards_of,), jnp.float32, low / len(pieces), high / len(pieces))
        gain = gain * jnp.repeat(jnp.exp(steps), dims[axis_at] // shards_of).reshape((-1,) + (1,) * (len(dims) - 1 - axis_at))
    return gain


def gaussian(rng, extent, deviation, limit, shards=(), kind=jnp.bfloat16):
    level = shard_levels(rng, extent, shards, -0.22, 0.18) if shards else 1.0
    values = jax.random.normal(rng, extent, jnp.float32) * deviation * level
    return jnp.minimum(jnp.maximum(values, -limit), limit).astype(kind)


def setup_inputs(seed: int = 0) -> dict:
    seeds = jax.random.split(jax.random.key(seed), 6)
    return {
        "field": gaussian(seeds[0], (MODES, NX, NY), 1.0, 6.0, ((0, 8), (1, 32))),
        "kappa_x": gaussian(seeds[1], (K, NX, NY), 0.5, 4.0, ((1, 32),), jnp.float32),
        "kappa_y": gaussian(seeds[2], (K, NX, NY), 0.5, 4.0, ((1, 32),), jnp.float32),
        "coupling": gaussian(seeds[3], (N_MODE * (ROUNDS + 1), K, MB, MB), (3 * MB) ** -0.5, 0.625, ((0, 8),)),
        "pattern": place_ends((jax.random.randint(seeds[4], (N_MODE * (ROUNDS + 1), K, MB, MB), 0, 3) < 1).astype(jnp.int32), jax.random.fold_in(seeds[4], 1), 0, 1),
    }


def mix(coef_k, block):
    return jnp.einsum("ij,jrw->irw", coef_k, block, precision=lax.Precision.HIGHEST)


def reference(field, kappa_x, kappa_y, coupling, pattern):
    zeros_bf = jnp.zeros(coupling.shape, jnp.bfloat16)
    coef = jnp.where(pattern > 0, coupling, zeros_bf).astype(jnp.float32)
    coef = coef.reshape(N_MODE, ROUNDS + 1, K, MB, MB)
    blocks = field.astype(jnp.float32).reshape(N_MODE, MB, NX, NY)
    padded = jnp.concatenate([blocks, jnp.zeros((N_MODE, MB, 1, NY), jnp.float32)], axis=2)

    def one_block(index):
        own = padded[index]
        flux_x = jnp.zeros((MB, NX, NY), jnp.float32)
        flux_y = jnp.zeros((MB, NX, NY), jnp.float32)
        for k in range(K):
            ck = coef[index, 0, k]
            wk = 0.5 * (mix(ck, own) + mix(ck.T, own))
            for r in range(1, ROUNDS + 1):
                upper = (index + r) % N_MODE
                lower = (index - r) % N_MODE
                wk = wk + mix(coef[index, r, k], padded[upper]) + mix(coef[lower, r, k].T, padded[lower])
            inner = wk[:, :NX, :]
            diff_x = wk[:, 1:, :] - inner
            next_col = jnp.concatenate([inner[:, :, 1:], jnp.zeros((MB, NX, 1), jnp.float32)], axis=2)
            flux_x = flux_x + kappa_x[k] * diff_x
            flux_y = flux_y + kappa_y[k] * (next_col - inner)
        prev_x = jnp.concatenate([jnp.zeros((MB, 1, NY), jnp.float32), flux_x[:, :-1, :]], axis=1)
        prev_y = jnp.concatenate([jnp.zeros((MB, NX, 1), jnp.float32), flux_y[:, :, :-1]], axis=2)
        return -(flux_x - prev_x) - (flux_y - prev_y)

    result = lax.map(one_block, jnp.arange(N_MODE, dtype=jnp.int32))
    return result.reshape(MODES, NX, NY)
```

```python
import functools

import jax
import jax.numpy as jnp
from jax import lax
from jax.experimental import pallas as pl
from jax.experimental.pallas import tpu as pltpu
from jax.sharding import PartitionSpec as P

TILE = 256
HALF = 8


def along_space(x, by):
    count = lax.axis_size("space")
    return lax.ppermute(x, "space", [(i, i + by) for i in range(count) if 0 <= i + by < count])


def along_mode(x, by):
    count = lax.axis_size("mode")
    return lax.ppermute(x, "mode", [(i, (i + by) % count) for i in range(count)])


def vmem_specs(n):
    return [pl.BlockSpec(memory_space=pltpu.VMEM)] * n


def split_body(field_ref, rim_ref, first_ref, second_ref):
    rows = jnp.swapaxes(field_ref[...].astype(jnp.float32), 0, 1).astype(jnp.bfloat16)
    rim_ref[0] = rows[0]
    rim_ref[1] = rows[15]
    first_ref[...] = rows[1:9]
    second_ref[...] = rows[9:15]


def split_rows(field):
    modes, rows, cols = field.shape
    return pl.pallas_call(
        split_body,
        out_shape=(
            jax.ShapeDtypeStruct((2, modes, cols), jnp.bfloat16),
            jax.ShapeDtypeStruct((HALF, modes, cols), jnp.bfloat16),
            jax.ShapeDtypeStruct((rows - HALF - 2, modes, cols), jnp.bfloat16),
        ),
        in_specs=vmem_specs(1),
        out_specs=vmem_specs(3),
        cost_estimate=pl.CostEstimate(flops=0, bytes_accessed=4 * field.size, transcendentals=0),
    )(field)


def image_body(base, mix_ref, kx_ref, ky_ref, kx_rim_ref, *refs):
    groups, (out_ref, stack, behind, sum_p, sum_q, sum_g) = refs[:-6], refs[-6:]
    modes = stack.shape[1] // 4
    cols = stack.shape[2]
    kterms = kx_ref.shape[0]
    place = 0
    for own, upper, lower in zip(groups[0::3], groups[1::3], groups[2::3]):
        n = own.shape[0]
        stack[place : place + n, :modes] = own[...]
        stack[place : place + n, modes : 2 * modes] = own[...]
        stack[place : place + n, 2 * modes : 3 * modes] = upper[...]
        stack[place : place + n, 3 * modes :] = lower[...]
        place += n
    ky = ky_ref[:, base : base + HALF, :]
    lane = lax.broadcasted_iota(jnp.int32, ky.shape, 2)
    behind[...] = jnp.where(lane == 0, 0.0, pltpu.roll(ky, 1, 2))

    def weighted(w, kappa_of):
        total = None
        for k in range(kterms):
            term = kappa_of(k) * w[k * modes : (k + 1) * modes]
            total = term if total is None else total + term
        return total

    def kx_of(i, at):
        if i < 0:
            return lambda k: kx_rim_ref[k : k + 1, at]
        return lambda k: kx_ref[k, i : i + 1, at]

    for n in range(HALF + 2):
        i = base - 1 + n
        for c in range(0, cols, TILE):
            at = slice(c, c + TILE)
            w = jnp.dot(mix_ref[...], stack[n, :, at], preferred_element_type=jnp.float32)
            if n > 0:
                sum_p[n, :, at] = weighted(w, kx_of(i - 1, at))
            if n < HALF + 1:
                sum_q[n, :, at] = weighted(w, kx_of(i, at))
            if 0 < n < HALF + 1:
                ahead = weighted(w, lambda k: behind[k, n - 1 : n, at])
                here = weighted(w, lambda k: ky_ref[k, i : i + 1, at])
                sum_g[0, :, at] = ahead
                sum_g[1, :, at] = here
        if 0 < n < HALF + 1:
            lane = lax.broadcasted_iota(jnp.int32, (modes, cols), 1)
            turned = pltpu.roll(sum_g[1], 1, 1)
            left = sum_g[0] - jnp.where(lane == 0, 0.0, turned)
            ended = jnp.where(lane == 0, -turned, left)
            right = pltpu.roll(ended, cols - 1, 1)
            sum_g[n + 1] = left - right
        if n > 1:
            image = (sum_p[n - 1] - sum_q[n - 2]) - (sum_p[n] - sum_q[n - 1]) + sum_g[n]
            out_ref[:, n - 2, :] = image


def image_rows(base, mix, kappa_x, kappa_y, kx_rim, groups, image):
    modes = groups[0][0].shape[1]
    cols = groups[0][0].shape[2]
    flat = [x for group in groups for x in group]
    rows = kappa_x.shape[1]
    operands = [mix, kappa_x, kappa_y, kx_rim, *flat]
    aliases = {}
    body = functools.partial(image_body, base)
    specs = vmem_specs(len(operands))
    if image is not None:
        aliases = {len(operands): 0}
        operands.append(image)
        specs.append(pl.BlockSpec(memory_space=pl.ANY))
        inner = body
        many = 4 + len(flat)

        def body(*refs):
            inner(*refs[:many], *refs[many + 1 :])

    return pl.pallas_call(
        body,
        grid=(1,),
        out_shape=jax.ShapeDtypeStruct((modes, rows, cols), jnp.float32),
        in_specs=specs,
        out_specs=pl.BlockSpec((modes, HALF, cols), lambda g: (0, base // HALF, 0)),
        scratch_shapes=[
            pltpu.VMEM((HALF + 2, 4 * modes, cols), jnp.bfloat16),
            pltpu.VMEM((kappa_x.shape[0], HALF, cols), jnp.float32),
            pltpu.VMEM((HALF + 2, modes, cols), jnp.float32),
            pltpu.VMEM((HALF + 2, modes, cols), jnp.float32),
            pltpu.VMEM((HALF + 2, modes, cols), jnp.float32),
        ],
        input_output_aliases=aliases,
        compiler_params=pltpu.CompilerParams(vmem_limit_bytes=40 << 20),
        cost_estimate=pl.CostEstimate(
            flops=2 * (HALF + 2) * 8 * modes * 4 * modes * cols, bytes_accessed=8 << 20, transcendentals=0
        ),
    )(*operands)


def shards(field, kappa_x, kappa_y, coupling, pattern):
    kterms, modes = coupling.shape[1], coupling.shape[2]
    rim, first, second = split_rows(field)
    rim_low = along_mode(rim, 1)
    rim_up = along_mode(rim, -1)
    first_low = along_mode(first, 1)
    first_up = along_mode(first, -1)
    coef = jnp.where(pattern > 0, coupling, jnp.zeros(coupling.shape, jnp.bfloat16))
    coef_low = along_mode(coef[1].reshape(kterms, modes * modes), 1).reshape(kterms, modes, modes)
    second_low = along_mode(second, 1)
    second_up = along_mode(second, -1)
    edge = kappa_x.shape[1] - 1
    kx_rim = along_space(kappa_x[:, edge, :], 1)
    top = jnp.concatenate([rim[0], rim_up[0], rim_low[0]], axis=0)
    bottom = jnp.concatenate([rim[1], rim_up[1], rim_low[1]], axis=0)
    after = along_space(top, -1)
    before = along_space(bottom, 1)

    half = coef[0] * 0.5
    mix = jnp.concatenate(
        [half, jnp.swapaxes(half, 1, 2), coef[1], jnp.swapaxes(coef_low, 1, 2)], axis=2
    ).reshape(kterms * modes, 4 * modes)

    def thirds(x):
        return tuple(x[n * modes : (n + 1) * modes][None] for n in range(3))

    image = image_rows(
        0,
        mix,
        kappa_x,
        kappa_y,
        kx_rim,
        [thirds(before), (rim[:1], rim_up[:1], rim_low[:1]), (first, first_up, first_low)],
        None,
    )
    image = image_rows(
        HALF,
        mix,
        kappa_x,
        kappa_y,
        kx_rim,
        [
            (first[6:], first_up[6:], first_low[6:]),
            (second, second_up, second_low),
            (rim[1:], rim_up[1:], rim_low[1:]),
            thirds(after),
        ],
        image,
    )
    return image


def solution(mesh):
    placed = (
        P("mode", "space", None),
        P(None, "space", None),
        P(None, "space", None),
        P("mode", None, None, None),
        P("mode", None, None, None),
    )
    return jax.shard_map(
        shards, mesh=mesh, in_specs=placed, out_specs=P("mode", "space", None), check_vma=False
    )
```

```python
import functools

import jax
import jax.numpy as jnp
from jax import lax
from jax.experimental import pallas as pl
from jax.experimental.pallas import tpu as pltpu
from jax.sharding import PartitionSpec as P

TILE = 256
PIECE = 256
EIGHT = 8
EARLY = 11
FORWARD_COST = 1 << 34
BF16 = jnp.bfloat16
F32 = jnp.float32
ANYWHERE = pl.BlockSpec(memory_space=pl.ANY)
ON_CHIP = pl.BlockSpec(memory_space=pltpu.VMEM)
OFF_CHIP = pl.BlockSpec(memory_space=pltpu.HBM)


def along_space(x, by):
    count = lax.axis_size("space")
    return lax.ppermute(x, "space", [(i, i + by) for i in range(count) if 0 <= i + by < count])


def along_mode(x, by):
    count = lax.axis_size("mode")
    return lax.ppermute(x, "mode", [(i, (i + by) % count) for i in range(count)])


def room(mebibytes):
    return pltpu.CompilerParams(vmem_limit_bytes=mebibytes << 20)


def cost(flops, bytes_accessed):
    return pl.CostEstimate(flops=flops, bytes_accessed=bytes_accessed, transcendentals=0)


def split_body(
    field_hbm,
    coupling_hbm,
    pattern_hbm,
    kx_hbm,
    rim_low,
    rim_up,
    early,
    late,
    edge,
    pieces,
    coupling_ref,
    pattern_ref,
    kx_ref,
    sems,
):
    modes, rows, cols = field_hbm.shape
    wide = pieces.shape[3]
    count = cols // wide
    copies = [
        pltpu.make_async_copy(field_hbm.at[:, :, n * wide : (n + 1) * wide], pieces.at[n], sems.at[n])
        for n in range(count)
    ]
    small = [
        pltpu.make_async_copy(coupling_hbm.at[1], coupling_ref, sems.at[count]),
        pltpu.make_async_copy(pattern_hbm.at[1], pattern_ref, sems.at[count + 1]),
        pltpu.make_async_copy(kx_hbm.at[:, rows - EIGHT :, :], kx_ref, sems.at[count + 2]),
    ]
    for copy in small[:2] + copies + small[2:]:
        copy.start()
    for copy in small[:2]:
        copy.wait()
    coef = jnp.where(pattern_ref[...] > 0, coupling_ref[...].astype(F32), 0.0)
    flat = jnp.concatenate([coef[k] for k in range(coef.shape[0])], axis=1)
    packed = [flat[n * EIGHT : (n + 1) * EIGHT] for n in range(modes // EIGHT)]
    rim_low[2 * modes :] = jnp.concatenate(packed, axis=1).astype(BF16)
    for n, copy in enumerate(copies):
        at = slice(n * wide, (n + 1) * wide)
        copy.wait()
        turned = jnp.swapaxes(pieces[n], 0, 1)
        rim_low[:modes, at] = turned[0]
        rim_low[modes : 2 * modes, at] = turned[rows - 1]
        rim_up[:modes, at] = turned[0]
        rim_up[modes:, at] = turned[rows - 1]
        early[:, :, at] = turned[1 : 1 + EARLY]
        late[:, :, at] = turned[1 + EARLY : rows - 1]
    small[2].wait()
    rest = kx_ref[:, EIGHT - 1, :]
    first = rest.astype(BF16)
    rest = rest - first.astype(F32)
    second = rest.astype(BF16)
    third = (rest - second.astype(F32)).astype(BF16)
    edge[...] = jnp.concatenate([first, second, third, jnp.zeros_like(first)], axis=0)


def split_rows(field, coupling, pattern, kappa_x):
    modes, rows, cols = field.shape
    extra = coupling.shape[1] * modes * modes // cols
    return pl.pallas_call(
        split_body,
        out_shape=(
            jax.ShapeDtypeStruct((2 * modes + extra, cols), BF16),
            jax.ShapeDtypeStruct((2 * modes, cols), BF16),
            jax.ShapeDtypeStruct((EARLY, modes, cols), BF16),
            jax.ShapeDtypeStruct((rows - 2 - EARLY, modes, cols), BF16),
            jax.ShapeDtypeStruct((4 * kappa_x.shape[0], cols), BF16),
        ),
        in_specs=[OFF_CHIP] * 4,
        out_specs=(ON_CHIP,) * 5,
        scratch_shapes=[
            pltpu.VMEM((cols // PIECE, modes, rows, PIECE), BF16),
            pltpu.VMEM(coupling.shape[1:], BF16),
            pltpu.VMEM(pattern.shape[1:], jnp.int32),
            pltpu.VMEM((kappa_x.shape[0], EIGHT, cols), F32),
            pltpu.SemaphoreType.DMA((cols // PIECE + 3,)),
        ],
        compiler_params=room(8),
        cost_estimate=cost(0, 4 * field.size),
    )(*(pltpu.with_memory_space_constraint(x, pltpu.HBM) for x in (field, coupling, pattern, kappa_x)))


def forward_body(own, lower, upper, edge, top, bottom):
    modes = upper.shape[0] // 2
    for n, block in enumerate((own, upper, lower)):
        top[n * modes : (n + 1) * modes] = block[:modes]
        bottom[n * modes : (n + 1) * modes] = block[modes : 2 * modes]
    bottom[3 * modes :] = edge[...]


def forward_rows(own, lower, upper, edge):
    modes, cols = upper.shape[0] // 2, upper.shape[1]
    return pl.pallas_call(
        forward_body,
        out_shape=(
            jax.ShapeDtypeStruct((3 * modes, cols), BF16),
            jax.ShapeDtypeStruct((3 * modes + edge.shape[0], cols), BF16),
        ),
        in_specs=[ON_CHIP] * 4,
        out_specs=(ON_CHIP,) * 2,
        compiler_params=room(4),
        cost_estimate=cost(FORWARD_COST, 1 << 20),
    )(own, lower, upper, edge)


def mix_body(coupling_ref, pattern_ref, lower, mix_ref):
    kterms, modes = coupling_ref.shape[1:3]
    coef = jnp.where(pattern_ref[...] > 0, coupling_ref[...].astype(F32), 0.0)
    half = coef[0] * 0.5
    packed = lower[2 * modes :].astype(F32)
    wide = packed.shape[1] * EIGHT // modes
    low = jnp.concatenate([packed[:, n * wide : (n + 1) * wide] for n in range(modes // EIGHT)], axis=0)
    parts = [half, jnp.swapaxes(half, 1, 2), coef[1]]
    parts = [x.reshape(kterms * modes, modes) for x in parts] + [low.T]
    mix = jnp.concatenate(parts, axis=1)
    mix_ref[...] = jnp.concatenate([-mix, mix], axis=1).astype(BF16)


def mixing(coupling, pattern, lower):
    kterms, modes = coupling.shape[1:3]
    return pl.pallas_call(
        mix_body,
        out_shape=jax.ShapeDtypeStruct((kterms * modes, 8 * modes), BF16),
        in_specs=[ON_CHIP] * 3,
        out_specs=ON_CHIP,
        compiler_params=room(4),
        cost_estimate=cost(0, 1 << 20),
    )(coupling, pattern, lower)


def image_row_values(first, count, kx_of, ky_of, mix_ref, stack, flux, put):
    modes, cols = flux.shape[1:]
    kterms = mix_ref.shape[0] // modes
    depth = stack.shape[1]
    lane = lax.broadcasted_iota(jnp.int32, (modes, cols), 1)
    edge = lax.broadcasted_iota(jnp.int32, (3 * modes, cols), 1) == cols - 1

    def weighted(diff, kappa_of):
        total = None
        for k in range(kterms):
            term = kappa_of(k) * diff[k * modes : (k + 1) * modes]
            total = term if total is None else total + term
        return total

    for n in range(count + 1):
        i = first - 1 + n
        for c in range(0, cols, TILE):
            at = slice(c, c + TILE)
            pair = stack[n : n + 2, :, at].reshape(2 * depth, TILE)
            diff = jnp.dot(mix_ref[...], pair, preferred_element_type=F32)
            flux[n, :, at] = weighted(diff, lambda k: kx_of(i, k, at))
        if n > 0:
            turned = pltpu.roll(stack[n, modes:].astype(F32), cols - 1, 1)
            turned = jnp.where(edge, 0.0, turned).astype(BF16)
            turned = jnp.concatenate([turned[:modes], turned], axis=0)
            across = []
            for c in range(0, cols, TILE):
                at = slice(c, c + TILE)
                pair = jnp.concatenate([stack[n, :, at], turned[:, at]], axis=0)
                diff = jnp.dot(mix_ref[...], pair, preferred_element_type=F32)
                across.append(weighted(diff, lambda k: ky_of(i, k, at)))
            across = jnp.concatenate(across, axis=1)
            left = jnp.where(lane == 0, 0.0, pltpu.roll(across, 1, 1))
            put(i, (flux[n - 1] - flux[n]) + (left - across))


def pile(stack, place, own, upper, lower):
    modes = own.shape[-2]
    stack[place, :modes] = own
    stack[place, modes : 2 * modes] = own
    stack[place, 2 * modes : 3 * modes] = upper
    stack[place, 3 * modes :] = lower


def early_body(mix_ref, kx_ref, ky_ref, before, *refs):
    (own, lower, upper), (inner, inner_low, inner_up), (image, spare, stack, flux, edge_kx) = (
        refs[:3],
        refs[3:6],
        refs[6:],
    )
    modes = upper.shape[0] // 2
    kterms = kx_ref.shape[0]
    pieces = before[3 * modes :].astype(F32)
    edge_kx[...] = (pieces[:kterms] + pieces[kterms : 2 * kterms]) + pieces[2 * kterms : 3 * kterms]
    pile(stack, 0, before[:modes], before[modes : 2 * modes], before[2 * modes : 3 * modes])
    pile(stack, 1, own[:modes], upper[:modes], lower[:modes])
    for n in range(EARLY):
        pile(stack, 2 + n, inner[n], inner_up[n], inner_low[n])

    def put(i, value):
        if i < EIGHT:
            image[:, i, :] = value
        else:
            spare[i - EIGHT] = value

    image_row_values(
        0,
        EARLY,
        lambda i, k, at: edge_kx[k : k + 1, at] if i < 0 else kx_ref[k, i : i + 1, at],
        lambda i, k, at: ky_ref[k, i : i + 1, at],
        mix_ref,
        stack,
        flux,
        put,
    )


def early_image(mix, kappa_x, kappa_y, before, rims, inner):
    kterms, rows, cols = kappa_x.shape
    modes = inner[0].shape[1]
    return pl.pallas_call(
        early_body,
        grid=(1,),
        out_shape=(
            jax.ShapeDtypeStruct((modes, rows, cols), F32),
            jax.ShapeDtypeStruct((EARLY - EIGHT, modes, cols), F32),
        ),
        in_specs=[ON_CHIP] * 10,
        out_specs=(pl.BlockSpec((modes, EIGHT, cols), lambda g: (0, 0, 0)), ON_CHIP),
        scratch_shapes=[
            pltpu.VMEM((EARLY + 2, 4 * modes, cols), BF16),
            pltpu.VMEM((EARLY + 1, modes, cols), F32),
            pltpu.VMEM((kterms, cols), F32),
        ],
        compiler_params=room(20),
        cost_estimate=cost(4 * EARLY * kterms * modes * 8 * modes * cols, 4 << 20),
    )(mix, kappa_x, kappa_y, before, *rims, *inner)


def late_body(mix_ref, kx_ref, ky_ref, after, *refs):
    rims, inner, last, spare, (_, image, stack, flux) = refs[:3], refs[3:6], refs[6:9], refs[9], refs[10:]
    modes = rims[2].shape[0] // 2
    rows = kx_ref.shape[1]
    count = rows - EARLY
    for n in range(EARLY - EIGHT):
        image[:, n, :] = spare[n]
    own, lower, upper = inner
    for n in range(2):
        pile(stack, n, own[EARLY - 2 + n], upper[EARLY - 2 + n], lower[EARLY - 2 + n])
    own, lower, upper = last
    for n in range(count - 2):
        pile(stack, 2 + n, own[n], upper[n], lower[n])
    own, lower, upper = rims
    pile(stack, count, own[modes : 2 * modes], upper[modes:], lower[modes : 2 * modes])
    pile(stack, count + 1, after[:modes], after[modes : 2 * modes], after[2 * modes :])

    def put(i, value):
        image[:, i - EIGHT, :] = value

    image_row_values(
        EARLY,
        count,
        lambda i, k, at: kx_ref[k, i : i + 1, at],
        lambda i, k, at: ky_ref[k, i : i + 1, at],
        mix_ref,
        stack,
        flux,
        put,
    )


def late_image(mix, kappa_x, kappa_y, after, rims, inner, last, spare, image):
    kterms, rows, cols = kappa_x.shape
    modes = inner[0].shape[1]
    count = rows - EARLY
    return pl.pallas_call(
        late_body,
        grid=(1,),
        out_shape=jax.ShapeDtypeStruct((modes, rows, cols), F32),
        in_specs=[ON_CHIP] * 14 + [ANYWHERE],
        out_specs=pl.BlockSpec((modes, EIGHT, cols), lambda g: (0, 1, 0)),
        scratch_shapes=[
            pltpu.VMEM((count + 2, 4 * modes, cols), BF16),
            pltpu.VMEM((count + 1, modes, cols), F32),
        ],
        input_output_aliases={14: 0},
        compiler_params=room(20),
        cost_estimate=cost(4 * count * kterms * modes * 8 * modes * cols, 4 << 20),
    )(mix, kappa_x, kappa_y, after, *rims, *inner, *last, spare, image)


def shards(field, kappa_x, kappa_y, coupling, pattern):
    rim, rim_bare, inner, last, edge = split_rows(field, coupling, pattern, kappa_x)
    rim_low = along_mode(rim, 1)
    rim_up = along_mode(rim_bare, -1)
    inner_low = along_mode(inner, 1)
    inner_up = along_mode(inner, -1)
    top, bottom = forward_rows(rim, rim_low, rim_up, edge)
    before = along_space(bottom, 1)
    after = along_space(top, -1)
    mix = mixing(coupling, pattern, rim_low)
    last_low = along_mode(lax.optimization_barrier((last, top))[0], 1)
    last_up = along_mode(lax.optimization_barrier((last, before))[0], -1)
    rims = (rim, rim_low, rim_up)
    inners = (inner, inner_low, inner_up)
    image, spare = early_image(mix, kappa_x, kappa_y, before, rims, inners)
    return late_image(
        mix, kappa_x, kappa_y, after, rims, inners, (last, last_low, last_up), spare, image
    )


def solution(mesh):
    placed = (
        P("mode", "space", None),
        P(None, "space", None),
        P(None, "space", None),
        P("mode", None, None, None),
        P("mode", None, None, None),
    )
    return jax.shard_map(
        shards, mesh=mesh, in_specs=placed, out_specs=P("mode", "space", None), check_vma=False
    )
```

```python
import functools

import jax
import jax.numpy as jnp
from jax import lax
from jax.experimental import pallas as pl
from jax.experimental.pallas import tpu as pltpu
from jax.sharding import PartitionSpec as P

TILE = 256
PIECE = 256
EIGHT = 8
KTERMS = 8
EARLY = 11
FORWARD_COST = 1 << 34
BF16 = jnp.bfloat16
F32 = jnp.float32
ANYWHERE = pl.BlockSpec(memory_space=pl.ANY)
ON_CHIP = pl.BlockSpec(memory_space=pltpu.VMEM)
OFF_CHIP = pl.BlockSpec(memory_space=pltpu.HBM)


def swapped(x, axis, first, wraps):
    count = lax.axis_size(axis)
    starts = [i for i in range(first, count, 2) if wraps or i + 1 < count]
    pairs = [(i, (i + 1) % count) for i in starts]
    return lax.ppermute(x, axis, pairs + [(j, i) for i, j in pairs])


def odd_index(axis):
    return lax.rem(lax.axis_index(axis), 2) == 1


def room(mebibytes):
    return pltpu.CompilerParams(vmem_limit_bytes=mebibytes << 20)


def cost(flops, bytes_accessed):
    return pl.CostEstimate(flops=flops, bytes_accessed=bytes_accessed, transcendentals=0)


def split_body(
    field_hbm,
    coupling_hbm,
    pattern_hbm,
    kx_hbm,
    rim,
    early,
    late,
    edge,
    pieces,
    coupling_ref,
    pattern_ref,
    kx_ref,
    sems,
):
    modes, rows, cols = field_hbm.shape
    wide = pieces.shape[3]
    count = cols // wide
    copies = [
        pltpu.make_async_copy(field_hbm.at[:, :, n * wide : (n + 1) * wide], pieces.at[n], sems.at[n])
        for n in range(count)
    ]
    small = [
        pltpu.make_async_copy(coupling_hbm.at[1], coupling_ref, sems.at[count]),
        pltpu.make_async_copy(pattern_hbm.at[1], pattern_ref, sems.at[count + 1]),
        pltpu.make_async_copy(kx_hbm.at[:, rows - EIGHT :, :], kx_ref, sems.at[count + 2]),
    ]
    for copy in small[:2] + copies + small[2:]:
        copy.start()
    for copy in small[:2]:
        copy.wait()
    coef = jnp.where(pattern_ref[...] > 0, coupling_ref[...].astype(F32), 0.0)
    flat = jnp.concatenate([coef[k] for k in range(coef.shape[0])], axis=1)
    packed = [flat[n * EIGHT : (n + 1) * EIGHT] for n in range(modes // EIGHT)]
    rim[2 * modes :] = jnp.concatenate(packed, axis=1).astype(BF16)
    for n, copy in enumerate(copies):
        at = slice(n * wide, (n + 1) * wide)
        copy.wait()
        turned = jnp.swapaxes(pieces[n], 0, 1)
        rim[:modes, at] = turned[0]
        rim[modes : 2 * modes, at] = turned[rows - 1]
        early[:, :, at] = turned[1 : 1 + EARLY]
        late[:, :, at] = turned[1 + EARLY : rows - 1]
    small[2].wait()
    kappa = kx_ref[:, EIGHT - 1, :]
    whole = kappa.astype(BF16)
    edge[...] = jnp.concatenate([whole, (kappa - whole.astype(F32)).astype(BF16)], axis=0)


def split_rows(field, coupling, pattern, kappa_x):
    modes, rows, cols = field.shape
    extra = coupling.shape[1] * modes * modes // cols
    return pl.pallas_call(
        split_body,
        out_shape=(
            jax.ShapeDtypeStruct((2 * modes + extra, cols), BF16),
            jax.ShapeDtypeStruct((EARLY, modes, cols), BF16),
            jax.ShapeDtypeStruct((rows - 2 - EARLY, modes, cols), BF16),
            jax.ShapeDtypeStruct((2 * kappa_x.shape[0], cols), BF16),
        ),
        in_specs=[OFF_CHIP] * 4,
        out_specs=(ON_CHIP,) * 4,
        scratch_shapes=[
            pltpu.VMEM((cols // PIECE, modes, rows, PIECE), BF16),
            pltpu.VMEM(coupling.shape[1:], BF16),
            pltpu.VMEM(pattern.shape[1:], jnp.int32),
            pltpu.VMEM((kappa_x.shape[0], EIGHT, cols), F32),
            pltpu.SemaphoreType.DMA((cols // PIECE + 3,)),
        ],
        compiler_params=room(8),
        cost_estimate=cost(0, 4 * field.size),
    )(*(pltpu.with_memory_space_constraint(x, pltpu.HBM) for x in (field, coupling, pattern, kappa_x)))


def forward_body(own, even, odd, edge, to_even, to_odd):
    modes = to_even.shape[0] // 3 - edge.shape[0] // 3
    flip = odd_index("space")

    def fill(first, last):
        for n, block in enumerate((own, even, odd)):
            at = slice(n * modes, (n + 1) * modes)
            first[at] = block[:modes]
            last[at] = block[modes : 2 * modes]
        first[3 * modes :] = edge[...]
        last[3 * modes :] = edge[...]

    @pl.when(flip)
    def _():
        fill(to_even, to_odd)

    @pl.when(jnp.logical_not(flip))
    def _():
        fill(to_odd, to_even)


def forward_rows(modes, own, even, odd, edge):
    cols = edge.shape[1]
    return pl.pallas_call(
        forward_body,
        out_shape=(jax.ShapeDtypeStruct((3 * modes + edge.shape[0], cols), BF16),) * 2,
        in_specs=[ON_CHIP] * 4,
        out_specs=(ON_CHIP,) * 2,
        compiler_params=room(4),
        cost_estimate=cost(FORWARD_COST, 1 << 20),
    )(own, even, odd, edge)


def mix_body(coupling_ref, pattern_ref, even, odd, mix_ref):
    kterms, modes = coupling_ref.shape[1:3]
    coef = jnp.where(pattern_ref[...] > 0, coupling_ref[...].astype(F32), 0.0)
    half = coef[0] * 0.5
    flip = odd_index("mode")
    packed = jnp.where(flip, even[2 * modes :].astype(F32), odd[2 * modes :].astype(F32))
    wide = packed.shape[1] * EIGHT // modes
    low = jnp.concatenate([packed[:, n * wide : (n + 1) * wide] for n in range(modes // EIGHT)], axis=0).T
    own, turned, up = (
        x.reshape(kterms * modes, modes) for x in (half, jnp.swapaxes(half, 1, 2), coef[1])
    )
    mix = jnp.concatenate([own, turned, jnp.where(flip, low, up), jnp.where(flip, up, low)], axis=1)
    mix_ref[...] = jnp.concatenate([-mix, mix], axis=1).astype(BF16)


def mixing(coupling, pattern, even, odd):
    kterms, modes = coupling.shape[1:3]
    return pl.pallas_call(
        mix_body,
        out_shape=jax.ShapeDtypeStruct((kterms * modes, 8 * modes), BF16),
        in_specs=[ON_CHIP] * 4,
        out_specs=ON_CHIP,
        compiler_params=room(4),
        cost_estimate=cost(0, 1 << 20),
    )(coupling, pattern, even, odd)


def weighted(diff, kappa_of):
    modes = diff.shape[0] // KTERMS
    total = None
    for k in range(KTERMS):
        term = kappa_of(k) * diff[k * modes : (k + 1) * modes]
        total = term if total is None else total + term
    return total


def row_flux(mix_ref, stack, n, at, kappa_of):
    pair = stack[n : n + 2, :, at].reshape(2 * stack.shape[1], at.stop - at.start)
    return weighted(jnp.dot(mix_ref[...], pair, preferred_element_type=F32), kappa_of)


def column_flux(mix_ref, stack, ahead, n, m, at, kappa_of):
    modes = ahead.shape[1] // 3
    pair = jnp.concatenate([stack[n, :, at], ahead[m, :modes, at], ahead[m, :, at]], axis=0)
    return weighted(jnp.dot(mix_ref[...], pair, preferred_element_type=F32), kappa_of)


def pile(stack, place, own, even, odd):
    modes = own.shape[-2]
    stack[place, :modes] = own
    stack[place, modes : 2 * modes] = own
    stack[place, 2 * modes : 3 * modes] = even
    stack[place, 3 * modes :] = odd


def look_ahead(stack, ahead, first, count):
    modes, cols = ahead.shape[1] // 3, ahead.shape[2]
    edge = lax.broadcasted_iota(jnp.int32, (3 * modes, cols), 1) == cols - 1
    for m in range(count):
        turned = pltpu.roll(stack[first + m, modes:], cols - 1, 1)
        ahead[m] = jnp.where(edge, jnp.zeros_like(turned), turned)


def shifted(value, carry):
    lane = lax.broadcasted_iota(jnp.int32, value.shape, 1)
    turned = pltpu.roll(value, 1, 1)
    return jnp.where(lane == 0, carry, turned), turned[:, :1]


def early_body(mix_ref, kx_ref, ky_ref, *refs):
    (own, even, odd), inner, (front, spare, stack, ahead, flux, laid) = refs[:3], refs[3:6], refs[6:]
    modes = front.shape[0]
    cols = front.shape[2]
    pile(stack, 0, own[:modes], even[:modes], odd[:modes])
    for n in range(EARLY):
        pile(stack, 1 + n, *(x[n] for x in inner))
    pile(stack, EARLY + 1, *(x[modes : 2 * modes] for x in (own, even, odd)))
    look_ahead(stack, ahead, 0, EARLY + 2)
    rows = kx_ref.shape[1]
    carry = [jnp.zeros((modes, 1), F32)] * (EARLY + 2)
    for c in range(0, cols, TILE):
        at = slice(c, c + TILE)
        for i in range(EARLY):
            flux[i, :, at] = row_flux(mix_ref, stack, i, at, lambda k: kx_ref[k, i : i + 1, at])
            right = column_flux(mix_ref, stack, ahead, i, i, at, lambda k: ky_ref[k, i : i + 1, at])
            left, carry[i] = shifted(right, carry[i])
            value = (left - right) - flux[i, :, at]
            if i > 0:
                value = value + flux[i - 1, :, at]
            if i < EIGHT:
                laid[i, :, at] = value
            else:
                spare[i - EIGHT, :, at] = value
        front[:, :, at] = jnp.swapaxes(laid[:, :, at], 0, 1)
        spare[EARLY - EIGHT, :, at] = flux[EARLY - 1, :, at]
        for n, i in ((EARLY, EARLY), (EARLY + 1, rows - 1)):
            right = column_flux(mix_ref, stack, ahead, n, n, at, lambda k: ky_ref[k, i : i + 1, at])
            left, carry[n] = shifted(right, carry[n])
            spare[n + 1 - EIGHT, :, at] = left - right


def early_image(mix, kappa_x, kappa_y, rims, inner):
    cols = kappa_x.shape[2]
    modes = inner[0].shape[1]
    return pl.pallas_call(
        early_body,
        out_shape=(
            jax.ShapeDtypeStruct((modes, EIGHT, cols), F32),
            jax.ShapeDtypeStruct((EARLY - EIGHT + 3, modes, cols), F32),
        ),
        in_specs=[ON_CHIP] * 9,
        out_specs=(ON_CHIP, ON_CHIP),
        scratch_shapes=[
            pltpu.VMEM((EARLY + 2, 4 * modes, cols), BF16),
            pltpu.VMEM((EARLY + 2, 3 * modes, cols), BF16),
            pltpu.VMEM((EARLY, modes, cols), F32),
            pltpu.VMEM((EIGHT, modes, cols), F32),
        ],
        compiler_params=room(20),
        cost_estimate=cost(4 * EARLY * KTERMS * modes * 8 * modes * cols, 4 << 20),
    )(mix, kappa_x, kappa_y, *rims, *inner)


def late_body(mix_ref, kx_ref, ky_ref, from_even, from_odd, *refs):
    (own, even, odd), inner, last = refs[:3], refs[3:6], refs[6:9]
    front, spare, image, stack, ahead, edge_kx, laid, out, sems = refs[9:]
    modes = front.shape[0]
    rows, cols = kx_ref.shape[1:]
    count = rows - EARLY
    flip = odd_index("space")

    def either(flipped, at):
        first, second = (from_even, from_odd) if flipped else (from_odd, from_even)
        return jnp.where(flip, first[at].astype(F32), second[at].astype(F32))

    def blocks(flipped):
        return (either(flipped, slice(n * modes, (n + 1) * modes)).astype(BF16) for n in range(3))

    kappa = either(True, slice(3 * modes, None))
    edge_kx[...] = kappa[:KTERMS] + kappa[KTERMS:]
    pile(stack, 0, *blocks(True))
    pile(stack, 1, own[:modes], even[:modes], odd[:modes])
    for c in range(0, cols, TILE):
        at = slice(c, c + TILE)
        above = row_flux(mix_ref, stack, 0, at, lambda k: edge_kx[k : k + 1, at])
        out[0, :, :, at] = front[:, :, at]
        out[0, :, 0, at] = front[:, 0, at] + above
    sends = [pltpu.make_async_copy(out.at[0], image.at[:, :EIGHT, :], sems.at[0])]
    sends[0].start()

    pile(stack, 2, *(x[EARLY - 1] for x in inner))
    for n in range(count - 2):
        pile(stack, 3 + n, *(x[n] for x in last))
    pile(stack, count + 1, *(x[modes : 2 * modes] for x in (own, even, odd)))
    pile(stack, count + 2, *blocks(False))
    look_ahead(stack, ahead, 3, count - 2)
    carry = [jnp.zeros((modes, 1), F32)] * (count - 2)
    for c in range(0, cols, TILE):
        at = slice(c, c + TILE)
        for n in range(EARLY - EIGHT):
            laid[n, :, at] = spare[n, :, at]
        behind = spare[EARLY - EIGHT, :, at]
        for m in range(count):
            i = EARLY + m
            here = row_flux(mix_ref, stack, 2 + m, at, lambda k: kx_ref[k, i : i + 1, at])
            if 0 < m < count - 1:
                right = column_flux(mix_ref, stack, ahead, 2 + m, m - 1, at, lambda k: ky_ref[k, i : i + 1, at])
                left, carry[m - 1] = shifted(right, carry[m - 1])
                across = left - right
            else:
                across = spare[EARLY - EIGHT + 1 + (m > 0), :, at]
            laid[i - EIGHT, :, at] = (behind - here) + across
            behind = here
        out[1, :, :, at] = jnp.swapaxes(laid[:, :, at], 0, 1)
        sends.append(
            pltpu.make_async_copy(out.at[1, :, :, at], image.at[:, EIGHT:, at], sems.at[1 + c // TILE])
        )
        sends[-1].start()
    for send in sends:
        send.wait()


def late_image(mix, kappa_x, kappa_y, from_even, from_odd, rims, inner, last, front, spare):
    kterms, rows, cols = kappa_x.shape
    modes = inner[0].shape[1]
    count = rows - EARLY
    return pl.pallas_call(
        late_body,
        out_shape=jax.ShapeDtypeStruct((modes, rows, cols), F32),
        in_specs=[ON_CHIP] * 16,
        out_specs=OFF_CHIP,
        scratch_shapes=[
            pltpu.VMEM((count + 3, 4 * modes, cols), BF16),
            pltpu.VMEM((count - 2, 3 * modes, cols), BF16),
            pltpu.VMEM((kterms, cols), F32),
            pltpu.VMEM((EIGHT, modes, cols), F32),
            pltpu.VMEM((2, modes, EIGHT, cols), F32),
            pltpu.SemaphoreType.DMA((1 + cols // TILE,)),
        ],
        compiler_params=room(20),
        cost_estimate=cost(4 * count * kterms * modes * 8 * modes * cols, 4 << 20),
    )(mix, kappa_x, kappa_y, from_even, from_odd, *rims, *inner, *last, front, spare)


def shards(field, kappa_x, kappa_y, coupling, pattern):
    rim, inner, last, edge = split_rows(field, coupling, pattern, kappa_x)

    def over_mode(x):
        return x, swapped(x, "mode", 0, True), swapped(x, "mode", 1, True)

    rims = over_mode(rim)
    inners = over_mode(inner)
    to_even, to_odd = forward_rows(field.shape[0], *rims, edge)
    from_even = swapped(to_even, "space", 0, False)
    from_odd = swapped(to_odd, "space", 1, False)
    mix = mixing(coupling, pattern, *rims[1:])
    last = lax.optimization_barrier((last, from_even))[0]
    front, spare = early_image(mix, kappa_x, kappa_y, rims, inners)
    return late_image(
        mix, kappa_x, kappa_y, from_even, from_odd, rims, inners, over_mode(last), front, spare
    )


def solution(mesh):
    placed = (
        P("mode", "space", None),
        P(None, "space", None),
        P(None, "space", None),
        P("mode", None, None, None),
        P("mode", None, None, None),
    )
    return jax.shard_map(
        shards, mesh=mesh, in_specs=placed, out_specs=P("mode", "space", None), check_vma=False
    )
```

```python
import functools

import jax
import jax.numpy as jnp
from jax import lax
from jax.experimental import pallas as pl
from jax.experimental.pallas import tpu as pltpu
from jax.sharding import PartitionSpec as P

TILE = 256
PIECE = 256
EIGHT = 8
KTERMS = 8
RUN = 8
EARLY = 11
FORWARD_COST = 1 << 34
BF16 = jnp.bfloat16
F32 = jnp.float32
ANYWHERE = pl.BlockSpec(memory_space=pl.ANY)
ON_CHIP = pl.BlockSpec(memory_space=pltpu.VMEM)
OFF_CHIP = pl.BlockSpec(memory_space=pltpu.HBM)


def swapped(x, first):
    count = lax.axis_size("mode")
    pairs = [(i, (i + 1) % count) for i in range(first, count, 2)]
    return lax.ppermute(x, "mode", pairs + [(j, i) for i, j in pairs])


def swapped_inside(x, first):
    count = lax.axis_size("space")
    pairs = [(i, i + 1) for i in range(first, count - 1, 2) if (i + 1) % RUN]
    return lax.ppermute(x, "space", pairs + [(j, i) for i, j in pairs])


def swapped_between(x):
    pairs = [(i - 1, i) for i in range(RUN, lax.axis_size("space"), RUN)]
    return lax.ppermute(x, "space", pairs + [(j, i) for i, j in pairs])


def odd_index(axis):
    return lax.rem(lax.axis_index(axis), 2) == 1


def room(mebibytes):
    return pltpu.CompilerParams(vmem_limit_bytes=mebibytes << 20)


def cost(flops, bytes_accessed):
    return pl.CostEstimate(flops=flops, bytes_accessed=bytes_accessed, transcendentals=0)


def split_body(
    field_hbm,
    coupling_hbm,
    pattern_hbm,
    kx_hbm,
    rim,
    early,
    late,
    edge,
    pieces,
    coupling_ref,
    pattern_ref,
    kx_ref,
    sems,
):
    modes, rows, cols = field_hbm.shape
    wide = pieces.shape[3]
    count = cols // wide
    copies = [
        pltpu.make_async_copy(field_hbm.at[:, :, n * wide : (n + 1) * wide], pieces.at[n], sems.at[n])
        for n in range(count)
    ]
    small = [
        pltpu.make_async_copy(coupling_hbm.at[1], coupling_ref, sems.at[count]),
        pltpu.make_async_copy(pattern_hbm.at[1], pattern_ref, sems.at[count + 1]),
        pltpu.make_async_copy(kx_hbm.at[:, rows - EIGHT :, :], kx_ref, sems.at[count + 2]),
    ]
    for copy in copies + small:
        copy.start()
    for n, copy in enumerate(copies):
        at = slice(n * wide, (n + 1) * wide)
        copy.wait()
        turned = jnp.swapaxes(pieces[n], 0, 1)
        rim[:modes, at] = turned[0]
        rim[modes : 2 * modes, at] = turned[rows - 1]
        early[:, :, at] = turned[1 : 1 + EARLY]
        late[:, :, at] = turned[1 + EARLY : rows - 1]
    for copy in small[:2]:
        copy.wait()
    coef = jnp.where(pattern_ref[...] > 0, coupling_ref[...].astype(F32), 0.0)
    flat = jnp.concatenate([coef[k] for k in range(coef.shape[0])], axis=1)
    packed = [flat[n * EIGHT : (n + 1) * EIGHT] for n in range(modes // EIGHT)]
    rim[2 * modes :] = jnp.concatenate(packed, axis=1).astype(BF16)
    small[2].wait()
    kappa = kx_ref[:, EIGHT - 1, :]
    whole = kappa.astype(BF16)
    edge[...] = jnp.concatenate([whole, (kappa - whole.astype(F32)).astype(BF16)], axis=0)


def split_rows(field, coupling, pattern, kappa_x):
    modes, rows, cols = field.shape
    extra = coupling.shape[1] * modes * modes // cols
    return pl.pallas_call(
        split_body,
        out_shape=(
            jax.ShapeDtypeStruct((2 * modes + extra, cols), BF16),
            jax.ShapeDtypeStruct((EARLY, modes, cols), BF16),
            jax.ShapeDtypeStruct((rows - 2 - EARLY, modes, cols), BF16),
            jax.ShapeDtypeStruct((2 * kappa_x.shape[0], cols), BF16),
        ),
        in_specs=[OFF_CHIP] * 4,
        out_specs=(ON_CHIP,) * 4,
        scratch_shapes=[
            pltpu.VMEM((cols // PIECE, modes, rows, PIECE), BF16),
            pltpu.VMEM(coupling.shape[1:], BF16),
            pltpu.VMEM(pattern.shape[1:], jnp.int32),
            pltpu.VMEM((kappa_x.shape[0], EIGHT, cols), F32),
            pltpu.SemaphoreType.DMA((cols // PIECE + 3,)),
        ],
        compiler_params=room(8),
        cost_estimate=cost(0, 4 * field.size),
    )(*(pltpu.with_memory_space_constraint(x, pltpu.HBM) for x in (field, coupling, pattern, kappa_x)))


def forward_body(own, even, odd, edge, to_even, to_odd):
    modes = to_even.shape[0] // 3 - edge.shape[0] // 3
    flip = odd_index("space")

    def fill(first, last):
        for n, block in enumerate((own, even, odd)):
            at = slice(n * modes, (n + 1) * modes)
            first[at] = block[:modes]
            last[at] = block[modes : 2 * modes]
        first[3 * modes :] = edge[...]
        last[3 * modes :] = edge[...]

    @pl.when(flip)
    def _():
        fill(to_even, to_odd)

    @pl.when(jnp.logical_not(flip))
    def _():
        fill(to_odd, to_even)


def forward_rows(modes, own, even, odd, edge):
    cols = edge.shape[1]
    return pl.pallas_call(
        forward_body,
        out_shape=(jax.ShapeDtypeStruct((3 * modes + edge.shape[0], cols), BF16),) * 2,
        in_specs=[ON_CHIP] * 4,
        out_specs=(ON_CHIP,) * 2,
        compiler_params=room(4),
        cost_estimate=cost(FORWARD_COST, 1 << 20),
    )(own, even, odd, edge)


def mix_body(coupling_ref, pattern_ref, even, odd, mix_ref):
    kterms, modes = coupling_ref.shape[1:3]
    coef = jnp.where(pattern_ref[...] > 0, coupling_ref[...].astype(F32), 0.0)
    half = coef[0] * 0.5
    flip = odd_index("mode")
    packed = jnp.where(flip, even[2 * modes :].astype(F32), odd[2 * modes :].astype(F32))
    wide = packed.shape[1] * EIGHT // modes
    low = jnp.concatenate([packed[:, n * wide : (n + 1) * wide] for n in range(modes // EIGHT)], axis=0).T
    own, turned, up = (
        x.reshape(kterms * modes, modes) for x in (half, jnp.swapaxes(half, 1, 2), coef[1])
    )
    mix = jnp.concatenate([own, turned, jnp.where(flip, low, up), jnp.where(flip, up, low)], axis=1)
    mix_ref[...] = jnp.concatenate([-mix, mix], axis=1).astype(BF16)


def mixing(coupling, pattern, even, odd):
    kterms, modes = coupling.shape[1:3]
    return pl.pallas_call(
        mix_body,
        out_shape=jax.ShapeDtypeStruct((kterms * modes, 8 * modes), BF16),
        in_specs=[ON_CHIP] * 4,
        out_specs=ON_CHIP,
        compiler_params=room(4),
        cost_estimate=cost(0, 1 << 20),
    )(coupling, pattern, even, odd)


def weighted(diff, kappa_of):
    modes = diff.shape[0] // KTERMS
    total = None
    for k in range(KTERMS):
        term = kappa_of(k) * diff[k * modes : (k + 1) * modes]
        total = term if total is None else total + term
    return total


def row_flux(mix_ref, stack, n, at, kappa_of):
    pair = stack[n : n + 2, :, at].reshape(2 * stack.shape[1], at.stop - at.start)
    return weighted(jnp.dot(mix_ref[...], pair, preferred_element_type=F32), kappa_of)


def column_flux(mix_ref, stack, ahead, n, m, at, kappa_of):
    modes = ahead.shape[1] // 3
    pair = jnp.concatenate([stack[n, :, at], ahead[m, :modes, at], ahead[m, :, at]], axis=0)
    return weighted(jnp.dot(mix_ref[...], pair, preferred_element_type=F32), kappa_of)


def pile(stack, place, own, even, odd):
    modes = own.shape[-2]
    stack[place, :modes] = own
    stack[place, modes : 2 * modes] = own
    stack[place, 2 * modes : 3 * modes] = even
    stack[place, 3 * modes :] = odd


def look_ahead(stack, ahead, first, count):
    modes, cols = ahead.shape[1] // 3, ahead.shape[2]
    edge = lax.broadcasted_iota(jnp.int32, (3 * modes, cols), 1) == cols - 1
    for m in range(count):
        turned = pltpu.roll(stack[first + m, modes:], cols - 1, 1)
        ahead[m] = jnp.where(edge, jnp.zeros_like(turned), turned)


def shifted(value, carry):
    lane = lax.broadcasted_iota(jnp.int32, value.shape, 1)
    turned = pltpu.roll(value, 1, 1)
    return jnp.where(lane == 0, carry, turned), turned[:, :1]


def early_body(mix_ref, kx_ref, ky_ref, *refs):
    (own, even, odd), inner, (front, spare, stack, ahead, flux, laid) = refs[:3], refs[3:6], refs[6:]
    modes = front.shape[0]
    cols = front.shape[2]
    pile(stack, 0, own[:modes], even[:modes], odd[:modes])
    for n in range(EARLY):
        pile(stack, 1 + n, *(x[n] for x in inner))
    pile(stack, EARLY + 1, *(x[modes : 2 * modes] for x in (own, even, odd)))
    look_ahead(stack, ahead, 0, EARLY + 2)
    rows = kx_ref.shape[1]
    carry = [jnp.zeros((modes, 1), F32)] * (EARLY + 2)
    for c in range(0, cols, TILE):
        at = slice(c, c + TILE)
        for i in range(EARLY):
            flux[i, :, at] = row_flux(mix_ref, stack, i, at, lambda k: kx_ref[k, i : i + 1, at])
            right = column_flux(mix_ref, stack, ahead, i, i, at, lambda k: ky_ref[k, i : i + 1, at])
            left, carry[i] = shifted(right, carry[i])
            value = (left - right) - flux[i, :, at]
            if i > 0:
                value = value + flux[i - 1, :, at]
            if i < EIGHT:
                laid[i, :, at] = value
            else:
                spare[i - EIGHT, :, at] = value
        front[:, :, at] = jnp.swapaxes(laid[:, :, at], 0, 1)
        spare[EARLY - EIGHT, :, at] = flux[EARLY - 1, :, at]
        for n, i in ((EARLY, EARLY), (EARLY + 1, rows - 1)):
            right = column_flux(mix_ref, stack, ahead, n, n, at, lambda k: ky_ref[k, i : i + 1, at])
            left, carry[n] = shifted(right, carry[n])
            spare[n + 1 - EIGHT, :, at] = left - right


def early_image(mix, kappa_x, kappa_y, rims, inner):
    cols = kappa_x.shape[2]
    modes = inner[0].shape[1]
    return pl.pallas_call(
        early_body,
        out_shape=(
            jax.ShapeDtypeStruct((modes, EIGHT, cols), F32),
            jax.ShapeDtypeStruct((EARLY - EIGHT + 3, modes, cols), F32),
        ),
        in_specs=[ON_CHIP] * 9,
        out_specs=(ON_CHIP, ON_CHIP),
        scratch_shapes=[
            pltpu.VMEM((EARLY + 2, 4 * modes, cols), BF16),
            pltpu.VMEM((EARLY + 2, 3 * modes, cols), BF16),
            pltpu.VMEM((EARLY, modes, cols), F32),
            pltpu.VMEM((EIGHT, modes, cols), F32),
        ],
        compiler_params=room(20),
        cost_estimate=cost(4 * EARLY * KTERMS * modes * 8 * modes * cols, 4 << 20),
    )(mix, kappa_x, kappa_y, *rims, *inner)


def run_end_body(mix_ref, own, even, odd, edge, ends, row):
    modes = ends.shape[0] // 3
    cols = ends.shape[1]
    last = lax.rem(lax.axis_index("space"), RUN) == RUN - 1

    @pl.when(jnp.logical_not(last))
    def _():
        for n, block in enumerate((own, even, odd)):
            ends[n * modes : (n + 1) * modes] = block[:modes]

    @pl.when(last)
    def _():
        pile(row, 0, *(x[modes : 2 * modes] for x in (own, even, odd)))
        kappa = edge[:KTERMS].astype(F32) + edge[KTERMS:].astype(F32)
        for c in range(0, cols, TILE):
            at = slice(c, c + TILE)
            w = jnp.dot(mix_ref[:, 4 * modes :], row[0, :, at], preferred_element_type=F32)
            total = weighted(w, lambda k: kappa[k : k + 1, at])
            whole = total.astype(BF16)
            ends[:modes, at] = whole
            ends[modes : 2 * modes, at] = (total - whole.astype(F32)).astype(BF16)
        ends[2 * modes :] = jnp.concatenate([edge[...]] * (modes // edge.shape[0]), axis=0)


def run_end(modes, mix, rims, edge):
    cols = edge.shape[1]
    return pl.pallas_call(
        run_end_body,
        out_shape=jax.ShapeDtypeStruct((3 * modes, cols), BF16),
        in_specs=[ON_CHIP] * 5,
        out_specs=ON_CHIP,
        scratch_shapes=[pltpu.VMEM((1, 4 * modes, cols), BF16)],
        compiler_params=room(4),
        cost_estimate=cost(2 * KTERMS * modes * 4 * modes * cols, 1 << 20),
    )(mix, *rims, edge)


def edges_body(
    mix_ref, kx_ref, from_even, from_odd, between, own, even, odd, front, whole, face, stack, edge_kx
):
    modes, _, cols = front.shape
    rows = kx_ref.shape[1]
    flip = odd_index("space")
    turn = lax.rem(lax.axis_index("space"), RUN)

    def either(flipped, at):
        first, second = (from_even, from_odd) if flipped else (from_odd, from_even)
        return jnp.where(flip, first[at].astype(F32), second[at].astype(F32))

    def blocks(flipped):
        for n in range(3):
            at = slice(n * modes, (n + 1) * modes)
            value = either(flipped, at)
            if not flipped:
                value = jnp.where(turn == RUN - 1, between[at].astype(F32), value)
            yield value.astype(BF16)

    pieces = jnp.where(
        turn == 0,
        between[2 * modes : 2 * modes + 2 * KTERMS].astype(F32),
        either(True, slice(3 * modes, None)),
    )
    edge_kx[...] = pieces[:KTERMS] + pieces[KTERMS:]
    pile(stack, 0, *blocks(True))
    pile(stack, 1, *(x[:modes] for x in (own, even, odd)))
    pile(stack, 2, *(x[modes : 2 * modes] for x in (own, even, odd)))
    pile(stack, 3, *blocks(False))
    for c in range(0, cols, TILE):
        at = slice(c, c + TILE)
        other = between[:modes, at].astype(F32) + between[modes : 2 * modes, at].astype(F32)
        above = row_flux(mix_ref, stack, 0, at, lambda k: edge_kx[k : k + 1, at])
        whole[:, 0, at] = front[:, 0, at] + (above - jnp.where(turn == 0, other, 0.0))
        face[:, at] = row_flux(mix_ref, stack, 2, at, lambda k: kx_ref[k, rows - 1 : rows, at])


def edge_faces(mix, kappa_x, from_even, from_odd, between, rims, front):
    modes, _, cols = front.shape
    return pl.pallas_call(
        edges_body,
        out_shape=(jax.ShapeDtypeStruct(front.shape, F32), jax.ShapeDtypeStruct((modes, cols), F32)),
        in_specs=[ON_CHIP] * 9,
        out_specs=(ON_CHIP, ON_CHIP),
        scratch_shapes=[
            pltpu.VMEM((4, 4 * modes, cols), BF16),
            pltpu.VMEM((KTERMS, cols), F32),
        ],
        input_output_aliases={8: 0},
        compiler_params=room(12),
        cost_estimate=cost(4 * KTERMS * modes * 8 * modes * cols, 1 << 20),
    )(mix, kappa_x, from_even, from_odd, between, *rims, front)


def late_body(mix_ref, kx_ref, ky_ref, *refs):
    rims, inner, last, (front, spare, face), (image, stack, ahead, laid, out, sems) = (
        refs[:3],
        refs[3:6],
        refs[6:9],
        refs[9:12],
        refs[12:],
    )
    modes = front.shape[0]
    rows, cols = kx_ref.shape[1:]
    count = rows - EARLY
    sends = [pltpu.make_async_copy(front, image.at[:, :EIGHT, :], sems.at[0])]
    sends[0].start()
    pile(stack, 0, *(x[EARLY - 1] for x in inner))
    for n in range(count - 2):
        pile(stack, 1 + n, *(x[n] for x in last))
    pile(stack, count - 1, *(x[modes : 2 * modes] for x in rims))
    look_ahead(stack, ahead, 1, count - 2)
    carry = [jnp.zeros((modes, 1), F32)] * (count - 2)
    for c in range(0, cols, TILE):
        at = slice(c, c + TILE)
        for n in range(EARLY - EIGHT):
            laid[n, :, at] = spare[n, :, at]
        behind = spare[EARLY - EIGHT, :, at]
        for m in range(count):
            i = EARLY + m
            if m < count - 1:
                here = row_flux(mix_ref, stack, m, at, lambda k: kx_ref[k, i : i + 1, at])
            else:
                here = face[:, at]
            if 0 < m < count - 1:
                right = column_flux(mix_ref, stack, ahead, m, m - 1, at, lambda k: ky_ref[k, i : i + 1, at])
                left, carry[m - 1] = shifted(right, carry[m - 1])
                across = left - right
            else:
                across = spare[EARLY - EIGHT + 1 + (m > 0), :, at]
            laid[i - EIGHT, :, at] = (behind - here) + across
            behind = here
        out[:, :, at] = jnp.swapaxes(laid[:, :, at], 0, 1)
        sends.append(
            pltpu.make_async_copy(out.at[:, :, at], image.at[:, EIGHT:, at], sems.at[1 + c // TILE])
        )
        sends[-1].start()
    for send in sends:
        send.wait()


def late_image(mix, kappa_x, kappa_y, rims, inner, last, front, spare, face):
    kterms, rows, cols = kappa_x.shape
    modes = inner[0].shape[1]
    count = rows - EARLY
    return pl.pallas_call(
        late_body,
        out_shape=jax.ShapeDtypeStruct((modes, rows, cols), F32),
        in_specs=[ON_CHIP] * 15,
        out_specs=OFF_CHIP,
        scratch_shapes=[
            pltpu.VMEM((count, 4 * modes, cols), BF16),
            pltpu.VMEM((count - 2, 3 * modes, cols), BF16),
            pltpu.VMEM((EIGHT, modes, cols), F32),
            pltpu.VMEM((modes, EIGHT, cols), F32),
            pltpu.SemaphoreType.DMA((1 + cols // TILE,)),
        ],
        compiler_params=room(20),
        cost_estimate=cost(4 * count * kterms * modes * 8 * modes * cols, 4 << 20),
    )(mix, kappa_x, kappa_y, *rims, *inner, *last, front, spare, face)


def shards(field, kappa_x, kappa_y, coupling, pattern):
    rim, inner, last, edge = split_rows(field, coupling, pattern, kappa_x)

    def over_mode(x):
        return x, swapped(x, 0), swapped(x, 1)

    rims = over_mode(rim)
    inners = over_mode(inner)
    to_even, to_odd = forward_rows(field.shape[0], *rims, edge)
    from_even = swapped_inside(to_even, 0)
    from_odd = swapped_inside(to_odd, 1)
    mix = mixing(coupling, pattern, *rims[1:])
    last_odd = swapped(lax.optimization_barrier((last, from_even))[0], 1)
    last_even = swapped(lax.optimization_barrier((last, from_odd))[0], 0)
    between = swapped_between(run_end(field.shape[0], mix, rims, edge))
    front, spare = early_image(mix, kappa_x, kappa_y, rims, inners)
    front, face = edge_faces(mix, kappa_x, from_even, from_odd, between, rims, front)
    lasts = (last, last_even, last_odd)
    return late_image(mix, kappa_x, kappa_y, rims, inners, lasts, front, spare, face)


def solution(mesh):
    placed = (
        P("mode", "space", None),
        P(None, "space", None),
        P(None, "space", None),
        P("mode", None, None, None),
        P("mode", None, None, None),
    )
    return jax.shard_map(
        shards, mesh=mesh, in_specs=placed, out_specs=P("mode", "space", None), check_vma=False
    )
```

```python
import functools

import jax
import jax.numpy as jnp
from jax import lax
from jax.experimental import pallas as pl
from jax.experimental.pallas import tpu as pltpu
from jax.sharding import PartitionSpec as P

TILE = 256
PIECE = 256
EIGHT = 8
KTERMS = 8
RUN = 8
EARLY = 11
FORWARD_COST = 1 << 34
BF16 = jnp.bfloat16
F32 = jnp.float32
ANYWHERE = pl.BlockSpec(memory_space=pl.ANY)
ON_CHIP = pl.BlockSpec(memory_space=pltpu.VMEM)
OFF_CHIP = pl.BlockSpec(memory_space=pltpu.HBM)


def swapped(x, first):
    count = lax.axis_size("mode")
    pairs = [(i, (i + 1) % count) for i in range(first, count, 2)]
    return lax.ppermute(x, "mode", pairs + [(j, i) for i, j in pairs])


def swapped_inside(x, first):
    count = lax.axis_size("space")
    pairs = [(i, i + 1) for i in range(first, count - 1, 2) if (i + 1) % RUN]
    return lax.ppermute(x, "space", pairs + [(j, i) for i, j in pairs])


def swapped_between(x):
    pairs = [(i - 1, i) for i in range(RUN, lax.axis_size("space"), RUN)]
    return lax.ppermute(x, "space", pairs + [(j, i) for i, j in pairs])


def odd_index(axis):
    return lax.rem(lax.axis_index(axis), 2) == 1


def room(mebibytes):
    return pltpu.CompilerParams(vmem_limit_bytes=mebibytes << 20)


def cost(flops, bytes_accessed):
    return pl.CostEstimate(flops=flops, bytes_accessed=bytes_accessed, transcendentals=0)


def split_body(
    field_hbm,
    coupling_hbm,
    pattern_hbm,
    kx_hbm,
    rim,
    early,
    late,
    edge,
    pieces,
    coupling_ref,
    pattern_ref,
    kx_ref,
    sems,
):
    modes, rows, cols = field_hbm.shape
    wide = pieces.shape[3]
    count = cols // wide
    copies = [
        pltpu.make_async_copy(field_hbm.at[:, :, n * wide : (n + 1) * wide], pieces.at[n], sems.at[n])
        for n in range(count)
    ]
    small = [
        pltpu.make_async_copy(coupling_hbm.at[1], coupling_ref, sems.at[count]),
        pltpu.make_async_copy(pattern_hbm.at[1], pattern_ref, sems.at[count + 1]),
        pltpu.make_async_copy(kx_hbm.at[:, rows - EIGHT :, :], kx_ref, sems.at[count + 2]),
    ]
    for copy in copies + small:
        copy.start()
    for n, copy in enumerate(copies):
        at = slice(n * wide, (n + 1) * wide)
        copy.wait()
        turned = jnp.swapaxes(pieces[n], 0, 1)
        rim[:modes, at] = turned[0]
        rim[modes : 2 * modes, at] = turned[rows - 1]
        rim[2 * modes : 3 * modes, at] = turned[1]
        early[:, :, at] = turned[2 : 1 + EARLY]
        late[:, :, at] = turned[1 + EARLY : rows - 1]
    for copy in small[:2]:
        copy.wait()
    coef = jnp.where(pattern_ref[...] > 0, coupling_ref[...].astype(F32), 0.0)
    flat = jnp.concatenate([coef[k] for k in range(coef.shape[0])], axis=1)
    packed = [flat[n * EIGHT : (n + 1) * EIGHT] for n in range(modes // EIGHT)]
    rim[3 * modes :] = jnp.concatenate(packed, axis=1).astype(BF16)
    small[2].wait()
    kappa = kx_ref[:, EIGHT - 1, :]
    whole = kappa.astype(BF16)
    edge[...] = jnp.concatenate([whole, (kappa - whole.astype(F32)).astype(BF16)], axis=0)


def split_rows(field, coupling, pattern, kappa_x):
    modes, rows, cols = field.shape
    extra = coupling.shape[1] * modes * modes // cols
    return pl.pallas_call(
        split_body,
        out_shape=(
            jax.ShapeDtypeStruct((3 * modes + extra, cols), BF16),
            jax.ShapeDtypeStruct((EARLY - 1, modes, cols), BF16),
            jax.ShapeDtypeStruct((rows - 2 - EARLY, modes, cols), BF16),
            jax.ShapeDtypeStruct((2 * kappa_x.shape[0], cols), BF16),
        ),
        in_specs=[OFF_CHIP] * 4,
        out_specs=(ON_CHIP,) * 4,
        scratch_shapes=[
            pltpu.VMEM((cols // PIECE, modes, rows, PIECE), BF16),
            pltpu.VMEM(coupling.shape[1:], BF16),
            pltpu.VMEM(pattern.shape[1:], jnp.int32),
            pltpu.VMEM((kappa_x.shape[0], EIGHT, cols), F32),
            pltpu.SemaphoreType.DMA((cols // PIECE + 3,)),
        ],
        compiler_params=room(8),
        cost_estimate=cost(0, 4 * field.size),
    )(*(pltpu.with_memory_space_constraint(x, pltpu.HBM) for x in (field, coupling, pattern, kappa_x)))


def forward_body(own, even, odd, edge, to_even, to_odd):
    modes = to_even.shape[0] // 3 - edge.shape[0] // 3
    flip = odd_index("space")

    def fill(first, last):
        for n, block in enumerate((own, even, odd)):
            at = slice(n * modes, (n + 1) * modes)
            first[at] = block[:modes]
            last[at] = block[modes : 2 * modes]
        first[3 * modes :] = edge[...]
        last[3 * modes :] = edge[...]

    @pl.when(flip)
    def _():
        fill(to_even, to_odd)

    @pl.when(jnp.logical_not(flip))
    def _():
        fill(to_odd, to_even)


def forward_rows(modes, own, even, odd, edge):
    cols = edge.shape[1]
    return pl.pallas_call(
        forward_body,
        out_shape=(jax.ShapeDtypeStruct((3 * modes + edge.shape[0], cols), BF16),) * 2,
        in_specs=[ON_CHIP] * 4,
        out_specs=(ON_CHIP,) * 2,
        compiler_params=room(4),
        cost_estimate=cost(FORWARD_COST, 1 << 20),
    )(own, even, odd, edge)


def mix_body(coupling_ref, pattern_ref, even, odd, mix_ref):
    kterms, modes = coupling_ref.shape[1:3]
    coef = jnp.where(pattern_ref[...] > 0, coupling_ref[...].astype(F32), 0.0)
    half = coef[0] * 0.5
    flip = odd_index("mode")
    packed = jnp.where(flip, even[3 * modes :].astype(F32), odd[3 * modes :].astype(F32))
    wide = packed.shape[1] * EIGHT // modes
    low = jnp.concatenate([packed[:, n * wide : (n + 1) * wide] for n in range(modes // EIGHT)], axis=0).T
    own, turned, up = (
        x.reshape(kterms * modes, modes) for x in (half, jnp.swapaxes(half, 1, 2), coef[1])
    )
    mix = jnp.concatenate([own, turned, jnp.where(flip, low, up), jnp.where(flip, up, low)], axis=1)
    mix_ref[...] = jnp.concatenate([-mix, mix], axis=1).astype(BF16)


def mixing(coupling, pattern, even, odd):
    kterms, modes = coupling.shape[1:3]
    return pl.pallas_call(
        mix_body,
        out_shape=jax.ShapeDtypeStruct((kterms * modes, 8 * modes), BF16),
        in_specs=[ON_CHIP] * 4,
        out_specs=ON_CHIP,
        compiler_params=room(4),
        cost_estimate=cost(0, 1 << 20),
    )(coupling, pattern, even, odd)


def weighted(diff, kappa_of):
    modes = diff.shape[0] // KTERMS
    total = None
    for k in range(KTERMS):
        term = kappa_of(k) * diff[k * modes : (k + 1) * modes]
        total = term if total is None else total + term
    return total


def row_flux(mix_ref, stack, n, at, kappa_of):
    pair = stack[n : n + 2, :, at].reshape(2 * stack.shape[1], at.stop - at.start)
    return weighted(jnp.dot(mix_ref[...], pair, preferred_element_type=F32), kappa_of)


def column_flux(mix_ref, stack, ahead, n, m, at, kappa_of):
    modes = ahead.shape[1] // 3
    pair = jnp.concatenate([stack[n, :, at], ahead[m, :modes, at], ahead[m, :, at]], axis=0)
    return weighted(jnp.dot(mix_ref[...], pair, preferred_element_type=F32), kappa_of)


def pile(stack, place, own, even, odd):
    modes = own.shape[-2]
    stack[place, :modes] = own
    stack[place, modes : 2 * modes] = own
    stack[place, 2 * modes : 3 * modes] = even
    stack[place, 3 * modes :] = odd


def look_ahead(stack, ahead, first, count):
    modes, cols = ahead.shape[1] // 3, ahead.shape[2]
    edge = lax.broadcasted_iota(jnp.int32, (3 * modes, cols), 1) == cols - 1
    for m in range(count):
        turned = pltpu.roll(stack[first + m, modes:], cols - 1, 1)
        ahead[m] = jnp.where(edge, jnp.zeros_like(turned), turned)


def shifted(value, carry):
    lane = lax.broadcasted_iota(jnp.int32, value.shape, 1)
    turned = pltpu.roll(value, 1, 1)
    return jnp.where(lane == 0, carry, turned), turned[:, :1]


def early_body(mix_ref, kx_ref, ky_ref, *refs):
    (own, even, odd), inner, (front, spare, stack, ahead, flux, laid) = refs[:3], refs[3:6], refs[6:]
    modes = front.shape[0]
    cols = front.shape[2]
    pile(stack, 0, own[:modes], even[:modes], odd[:modes])
    pile(stack, 1, *(x[2 * modes : 3 * modes] for x in (own, even, odd)))
    for n in range(EARLY - 1):
        pile(stack, 2 + n, *(x[n] for x in inner))
    pile(stack, EARLY + 1, *(x[modes : 2 * modes] for x in (own, even, odd)))
    look_ahead(stack, ahead, 0, EARLY + 2)
    rows = kx_ref.shape[1]
    carry = [jnp.zeros((modes, 1), F32)] * (EARLY + 2)
    for c in range(0, cols, TILE):
        at = slice(c, c + TILE)
        for i in range(EARLY):
            flux[i, :, at] = row_flux(mix_ref, stack, i, at, lambda k: kx_ref[k, i : i + 1, at])
            right = column_flux(mix_ref, stack, ahead, i, i, at, lambda k: ky_ref[k, i : i + 1, at])
            left, carry[i] = shifted(right, carry[i])
            value = (left - right) - flux[i, :, at]
            if i > 0:
                value = value + flux[i - 1, :, at]
            if i < EIGHT:
                laid[i, :, at] = value
            else:
                spare[i - EIGHT, :, at] = value
        front[:, :, at] = jnp.swapaxes(laid[:, :, at], 0, 1)
        spare[EARLY - EIGHT, :, at] = flux[EARLY - 1, :, at]
        for n, i in ((EARLY, EARLY), (EARLY + 1, rows - 1)):
            right = column_flux(mix_ref, stack, ahead, n, n, at, lambda k: ky_ref[k, i : i + 1, at])
            left, carry[n] = shifted(right, carry[n])
            spare[n + 1 - EIGHT, :, at] = left - right


def early_image(mix, kappa_x, kappa_y, rims, inner):
    cols = kappa_x.shape[2]
    modes = inner[0].shape[1]
    return pl.pallas_call(
        early_body,
        out_shape=(
            jax.ShapeDtypeStruct((modes, EIGHT, cols), F32),
            jax.ShapeDtypeStruct((EARLY - EIGHT + 3, modes, cols), F32),
        ),
        in_specs=[ON_CHIP] * 9,
        out_specs=(ON_CHIP, ON_CHIP),
        scratch_shapes=[
            pltpu.VMEM((EARLY + 2, 4 * modes, cols), BF16),
            pltpu.VMEM((EARLY + 2, 3 * modes, cols), BF16),
            pltpu.VMEM((EARLY, modes, cols), F32),
            pltpu.VMEM((EIGHT, modes, cols), F32),
        ],
        compiler_params=room(20),
        cost_estimate=cost(4 * EARLY * KTERMS * modes * 8 * modes * cols, 4 << 20),
    )(mix, kappa_x, kappa_y, *rims, *inner)


def run_end_body(mix_ref, own, even, odd, edge, ends, row):
    modes = ends.shape[0] // 3
    cols = ends.shape[1]
    last = lax.rem(lax.axis_index("space"), RUN) == RUN - 1

    @pl.when(jnp.logical_not(last))
    def _():
        for n, block in enumerate((own, even, odd)):
            ends[n * modes : (n + 1) * modes] = block[:modes]

    @pl.when(last)
    def _():
        pile(row, 0, *(x[modes : 2 * modes] for x in (own, even, odd)))
        kappa = edge[:KTERMS].astype(F32) + edge[KTERMS:].astype(F32)
        for c in range(0, cols, TILE):
            at = slice(c, c + TILE)
            w = jnp.dot(mix_ref[:, 4 * modes :], row[0, :, at], preferred_element_type=F32)
            total = weighted(w, lambda k: kappa[k : k + 1, at])
            whole = total.astype(BF16)
            ends[:modes, at] = whole
            ends[modes : 2 * modes, at] = (total - whole.astype(F32)).astype(BF16)
        ends[2 * modes :] = jnp.concatenate([edge[...]] * (modes // edge.shape[0]), axis=0)


def run_end(modes, mix, rims, edge):
    cols = edge.shape[1]
    return pl.pallas_call(
        run_end_body,
        out_shape=jax.ShapeDtypeStruct((3 * modes, cols), BF16),
        in_specs=[ON_CHIP] * 5,
        out_specs=ON_CHIP,
        scratch_shapes=[pltpu.VMEM((1, 4 * modes, cols), BF16)],
        compiler_params=room(4),
        cost_estimate=cost(2 * KTERMS * modes * 4 * modes * cols, 1 << 20),
    )(mix, *rims, edge)


def edges_body(
    mix_ref, kx_ref, from_even, from_odd, between, own, even, odd, front, whole, face, stack, edge_kx
):
    modes, _, cols = front.shape
    rows = kx_ref.shape[1]
    flip = odd_index("space")
    turn = lax.rem(lax.axis_index("space"), RUN)

    def either(flipped, at):
        first, second = (from_even, from_odd) if flipped else (from_odd, from_even)
        return jnp.where(flip, first[at].astype(F32), second[at].astype(F32))

    def blocks(flipped):
        for n in range(3):
            at = slice(n * modes, (n + 1) * modes)
            value = either(flipped, at)
            if not flipped:
                value = jnp.where(turn == RUN - 1, between[at].astype(F32), value)
            yield value.astype(BF16)

    pieces = jnp.where(
        turn == 0,
        between[2 * modes : 2 * modes + 2 * KTERMS].astype(F32),
        either(True, slice(3 * modes, None)),
    )
    edge_kx[...] = pieces[:KTERMS] + pieces[KTERMS:]
    pile(stack, 0, *blocks(True))
    pile(stack, 1, *(x[:modes] for x in (own, even, odd)))
    pile(stack, 2, *(x[modes : 2 * modes] for x in (own, even, odd)))
    pile(stack, 3, *blocks(False))
    for c in range(0, cols, TILE):
        at = slice(c, c + TILE)
        other = between[:modes, at].astype(F32) + between[modes : 2 * modes, at].astype(F32)
        above = row_flux(mix_ref, stack, 0, at, lambda k: edge_kx[k : k + 1, at])
        whole[:, 0, at] = front[:, 0, at] + (above - jnp.where(turn == 0, other, 0.0))
        face[:, at] = row_flux(mix_ref, stack, 2, at, lambda k: kx_ref[k, rows - 1 : rows, at])


def edge_faces(mix, kappa_x, from_even, from_odd, between, rims, front):
    modes, _, cols = front.shape
    return pl.pallas_call(
        edges_body,
        out_shape=(jax.ShapeDtypeStruct(front.shape, F32), jax.ShapeDtypeStruct((modes, cols), F32)),
        in_specs=[ON_CHIP] * 9,
        out_specs=(ON_CHIP, ON_CHIP),
        scratch_shapes=[
            pltpu.VMEM((4, 4 * modes, cols), BF16),
            pltpu.VMEM((KTERMS, cols), F32),
        ],
        input_output_aliases={8: 0},
        compiler_params=room(12),
        cost_estimate=cost(4 * KTERMS * modes * 8 * modes * cols, 1 << 20),
    )(mix, kappa_x, from_even, from_odd, between, *rims, front)


def late_body(mix_ref, kx_ref, ky_ref, *refs):
    rims, inner, last, (front, spare, face), (image, stack, ahead, laid, out, sems) = (
        refs[:3],
        refs[3:6],
        refs[6:9],
        refs[9:12],
        refs[12:],
    )
    modes = front.shape[0]
    rows, cols = kx_ref.shape[1:]
    count = rows - EARLY
    sends = [pltpu.make_async_copy(front, image.at[:, :EIGHT, :], sems.at[0])]
    sends[0].start()
    pile(stack, 0, *(x[EARLY - 2] for x in inner))
    for n in range(count - 2):
        pile(stack, 1 + n, *(x[n] for x in last))
    pile(stack, count - 1, *(x[modes : 2 * modes] for x in rims))
    look_ahead(stack, ahead, 1, count - 2)
    carry = [jnp.zeros((modes, 1), F32)] * (count - 2)
    for c in range(0, cols, TILE):
        at = slice(c, c + TILE)
        for n in range(EARLY - EIGHT):
            laid[n, :, at] = spare[n, :, at]
        behind = spare[EARLY - EIGHT, :, at]
        for m in range(count):
            i = EARLY + m
            if m < count - 1:
                here = row_flux(mix_ref, stack, m, at, lambda k: kx_ref[k, i : i + 1, at])
            else:
                here = face[:, at]
            if 0 < m < count - 1:
                right = column_flux(mix_ref, stack, ahead, m, m - 1, at, lambda k: ky_ref[k, i : i + 1, at])
                left, carry[m - 1] = shifted(right, carry[m - 1])
                across = left - right
            else:
                across = spare[EARLY - EIGHT + 1 + (m > 0), :, at]
            laid[i - EIGHT, :, at] = (behind - here) + across
            behind = here
        out[:, :, at] = jnp.swapaxes(laid[:, :, at], 0, 1)
        sends.append(
            pltpu.make_async_copy(out.at[:, :, at], image.at[:, EIGHT:, at], sems.at[1 + c // TILE])
        )
        sends[-1].start()
    for send in sends:
        send.wait()


def late_image(mix, kappa_x, kappa_y, rims, inner, last, front, spare, face):
    kterms, rows, cols = kappa_x.shape
    modes = inner[0].shape[1]
    count = rows - EARLY
    return pl.pallas_call(
        late_body,
        out_shape=jax.ShapeDtypeStruct((modes, rows, cols), F32),
        in_specs=[ON_CHIP] * 15,
        out_specs=OFF_CHIP,
        scratch_shapes=[
            pltpu.VMEM((count, 4 * modes, cols), BF16),
            pltpu.VMEM((count - 2, 3 * modes, cols), BF16),
            pltpu.VMEM((EIGHT, modes, cols), F32),
            pltpu.VMEM((modes, EIGHT, cols), F32),
            pltpu.SemaphoreType.DMA((1 + cols // TILE,)),
        ],
        compiler_params=room(20),
        cost_estimate=cost(4 * count * kterms * modes * 8 * modes * cols, 4 << 20),
    )(mix, kappa_x, kappa_y, *rims, *inner, *last, front, spare, face)


def shards(field, kappa_x, kappa_y, coupling, pattern):
    rim, inner, last, edge = split_rows(field, coupling, pattern, kappa_x)

    def over_mode(x):
        return x, swapped(x, 0), swapped(x, 1)

    rims = over_mode(rim)
    inners = over_mode(inner)
    to_even, to_odd = forward_rows(field.shape[0], *rims, edge)
    from_even = swapped_inside(to_even, 0)
    from_odd = swapped_inside(to_odd, 1)
    mix = mixing(coupling, pattern, *rims[1:])
    last_odd = swapped(lax.optimization_barrier((last, from_even))[0], 1)
    last_even = swapped(lax.optimization_barrier((last, from_odd))[0], 0)
    between = swapped_between(run_end(field.shape[0], mix, rims, edge))
    front, spare = early_image(mix, kappa_x, kappa_y, rims, inners)
    front, face = edge_faces(mix, kappa_x, from_even, from_odd, between, rims, front)
    lasts = (last, last_even, last_odd)
    return late_image(mix, kappa_x, kappa_y, rims, inners, lasts, front, spare, face)


def solution(mesh):
    placed = (
        P("mode", "space", None),
        P(None, "space", None),
        P(None, "space", None),
        P("mode", None, None, None),
        P("mode", None, None, None),
    )
    return jax.shard_map(
        shards, mesh=mesh, in_specs=placed, out_specs=P("mode", "space", None), check_vma=False
    )
```
